32 devices in a mesh: dp: 8 (over y, x, core), fsdp: 4 (over z).
Axes of the slice: x: 2, y: 2, z: 4, core: 2. Of those that a mesh axis runs over, the one named last changes fastest.
Arguments:
- gradients: bfloat16 [8, 512, 8192], P('dp', None, 'fsdp'), may hold values from -1.5 to 1.5
- momentum: float32 [512, 8192], P('dp', 'fsdp'), may hold values from -1500 to 1500
- weight: float32 [512, 8192], P(None, 'fsdp'), may hold values from -3 to 3
- logit_peaks: int32 [32, 32], P(('dp', 'fsdp')), may hold values from 0 to 479, as said below
- clip_threshold: int32 [1], replicated, may hold values from 60 to 120
Outputs:
- new_weight: float32 [512, 8192], P(None, 'fsdp')
- new_momentum: float32 [512, 8192], P('dp', 'fsdp')
- update_norm: float32 [1], replicated
The draws below stay inside these ranges and needn't reach their ends.
Inputs may be any that keep to these rules, and one draw needn't show every extreme that they name: `logit_peaks`: for every head, the largest entry over all rows is at least 40.
All inputs are finite; a program needn't handle non-finite values.
Results may differ from the reference program's by a relative error of at most 0.0023.
Values may be sent and summed in bfloat16 or wider, within the bound.
A program may use at most 64 MiB of HBM per device.

```python
import math
import jax
import jax.numpy as jnp
from jax import lax

KVL = 512
NOPE = 128
VDIM = 128
HEADS = 32
ITERS = 3
KVO = 8192
N_DP = 8
N_FSDP = 4


def draw_logit_peaks(key, part):
    first, second, third, fourth = jax.random.split(key, 4)
    device_count = N_DP * N_FSDP
    head_index = jnp.arange(HEADS)
    ceilings = jax.random.randint(first, (HEADS,), 40, 480)
    shuffled = jax.random.permutation(second, HEADS)
    ceilings = jnp.where(head_index == shuffled[0], 479, jnp.where(head_index == shuffled[1], 40, ceilings))
    holders = jax.random.randint(third, (HEADS,), 0, device_count)
    lesser = jax.random.randint(fourth, (device_count, HEADS), 0, 1048576) % (ceilings // 3 + 1)[None, :]
    row_index = jnp.arange(device_count)[:, None]
    return jnp.where(row_index == holders[None, :], ceilings[None, :], lesser).astype(jnp.int32)


def draw_momentum(key, part):
    first = jax.random.fold_in(key, 0)
    third = jax.random.fold_in(key, 2)
    noise = jax.random.truncated_normal(first, -4.0, 4.0, (KVL, KVO), jnp.float32)
    row_pos = jnp.arange(KVL, dtype=jnp.float32) / (KVL - 1)
    row_scale = jnp.exp(row_pos * 2.302585)[:, None]
    block_cols = KVO // (N_FSDP * N_DP)
    col_index = jnp.arange(KVO)
    block_index = col_index % (KVO // N_FSDP) // block_cols
    block_levels = jnp.exp(jax.random.uniform(third, (N_DP,), jnp.float32) * 2.0794415)
    block_scale = block_levels[block_index][None, :]
    values = row_scale * block_scale * noise
    return values.astype(jnp.float32)


def raised(entries, stream_key, source, target, shards_of, factor):
    owner, partner = [(jnp.arange(entries.shape[position]) // (entries.shape[position] // shards_of)).reshape([-1 if axis == position else 1 for axis in range(entries.ndim)]) for position in (source, target)]
    chosen = jax.random.permutation(stream_key, shards_of)[partner]
    strong = (owner == chosen) | (owner == (partner + shards_of // 2) % shards_of)
    return jnp.where(strong, factor * entries, entries)


def level_of(own_key, shape, pieces, least, high):
    def one(axis_at, shards_of):
        steps = jax.random.uniform(jax.random.fold_in(jax.random.fold_in(own_key, 6), axis_at), (shards_of,), jnp.float32, least / len(pieces), high / len(pieces))
        return jnp.repeat(jnp.exp(steps), shape[axis_at] // shards_of).reshape((-1,) + (1,) * (len(shape) - axis_at - 1))

    factor_of = one(*pieces[0])
    for cut in pieces[1:]:
        factor_of = factor_of * one(*cut)
    return factor_of


def bell_draw(own_key, shape, spread, limit, cuts=(), held_as=jnp.bfloat16):
    factor_of = level_of(own_key, shape, cuts, -0.22, 0.18) if cuts else 1.0
    result = jax.random.normal(own_key, shape, jnp.float32) * spread * factor_of
    return jnp.minimum(jnp.maximum(result, -limit), limit).astype(held_as)


def bell_draw_with(key, dims, deviation, most, cuts, heavy, kind=jnp.bfloat16):
    result = deviation * jax.random.normal(key, dims, jnp.float32)
    if cuts:
        result = result * level_of(key, dims, cuts, -0.22, 0.18)
    return jnp.clip(raised(result, jax.random.fold_in(key, 3), *heavy), -most, most).astype(kind)


def setup_inputs(seed: int = 0) -> dict:
    streams_of = jax.random.split(jax.random.key(seed), 6)
    gradients = bell_draw_with(streams_of[0], (N_DP, KVL, KVO), 0.25, 1.5, ((0, 8), (2, 4)), (0, 1, 8, 2.0))
    momentum = draw_momentum(jax.random.fold_in(streams_of[5], 71), 0)
    weight = bell_draw(streams_of[2], (KVL, KVO), 0.5, 3.0, ((1, 4),), jnp.float32)
    logit_peaks = draw_logit_peaks(jax.random.fold_in(streams_of[5], 71), 0)
    clip_threshold = jax.random.randint(streams_of[4], (1,), 60, 121).astype(jnp.int32)
    return {"gradients": gradients, "momentum": momentum, "weight": weight, "logit_peaks": logit_peaks, "clip_threshold": clip_threshold}


quintic_terms = (3.4445, -4.775, 2.0315)
learning_rate = 0.5
weight_decay = 0.1
momentum_decay = 0.95
update_gain = 0.2
epsilon = 1e-07

def column_factors(global_peaks, clip_threshold):
    largest = lax.optimization_barrier(jnp.max(global_peaks, axis=0)).astype(jnp.float32)
    clip_ratio = jnp.minimum(1.0, clip_threshold.astype(jnp.float32)[0] / largest)
    key_scale = jnp.sqrt(clip_ratio)
    per_head = jnp.concatenate([jnp.broadcast_to(key_scale[:, None], (HEADS, NOPE)), jnp.ones((HEADS, VDIM), jnp.float32)], axis=1)
    return per_head.reshape(HEADS * (NOPE + VDIM))

def orthogonalize(matrix):
    current = matrix
    for iteration in range(ITERS):
        square = lax.dot_general(current, current, (((1,), (1,)), ((), ())), precision=lax.Precision.HIGHEST, preferred_element_type=jnp.float32)
        combined = quintic_terms[1] * square + quintic_terms[2] * jnp.dot(square, square, precision=lax.Precision.HIGHEST, preferred_element_type=jnp.float32)
        current = quintic_terms[0] * current + jnp.dot(combined, current, precision=lax.Precision.HIGHEST, preferred_element_type=jnp.float32)
    return current

def reference(gradients, momentum, weight, logit_peaks, clip_threshold):
    summed = lax.optimization_barrier(jnp.sum(gradients.astype(jnp.float32), axis=0))
    new_momentum = momentum_decay * momentum + summed
    blended = summed + momentum_decay * new_momentum
    square_total = jnp.sum(blended * blended)
    update_norm = jnp.sqrt(square_total / (KVL * KVO)).reshape(1).astype(jnp.float32)
    normalized = blended / (jnp.sqrt(square_total) + epsilon)
    orthogonal = orthogonalize(normalized)
    update_scale = update_gain * math.sqrt(max(KVL, KVO))
    stepped = weight - learning_rate * (update_scale * orthogonal + weight_decay * weight)
    new_weight = stepped * column_factors(logit_peaks, clip_threshold)[None, :]
    return (new_weight, new_momentum, update_norm)
```

```python
import functools
import math

import jax
import jax.numpy as jnp
from jax import lax
from jax.experimental import pallas as pl
from jax.experimental.pallas import tpu as pltpu
from jax.sharding import PartitionSpec as P

KVL = 512
NOPE = 128
VDIM = 128
HEADS = 32
ITERS = 3
KVO = 8192


quintic_terms = (3.4445, -4.775, 2.0315)
learning_rate = 0.5
weight_decay = 0.1
momentum_decay = 0.95
update_gain = 0.2
epsilon = 1e-07


def head_factors(largest, clip_threshold):
    clip_ratio = jnp.minimum(1.0, clip_threshold.astype(jnp.float32)[0] / largest)
    key_scale = jnp.sqrt(clip_ratio)
    per_head = jnp.concatenate(
        [jnp.broadcast_to(key_scale[:, None], (HEADS, NOPE)), jnp.ones((HEADS, VDIM), jnp.float32)],
        axis=1,
    )
    return per_head.reshape(HEADS * (NOPE + VDIM))


def product(left, right):
    return jnp.dot(left, right, precision=lax.Precision.HIGH, preferred_element_type=jnp.float32)


def polynomial_of_gram(gram):
    lead, second, third = quintic_terms
    whole = None
    for iteration in range(ITERS):
        rest = second * gram + third * product(gram, gram)
        if whole is None:
            whole = lead * jnp.eye(KVL, dtype=jnp.float32) + rest
        else:
            whole = lead * whole + product(rest, whole)
        if iteration < ITERS - 1:
            half = lead * gram + product(rest, gram)
            gram = lead * half + product(half, rest)
    return whole


CHUNKS = 2
MESH = pl.DeviceIdType.MESH


def exchange(
    dp_count,
    fsdp_count,
    grad,
    momentum,
    peaks,
    new_momentum,
    columns,
    gram,
    stats_out,
    pair,
    outgoing,
    incoming,
    gram_own,
    gram_in,
    stats,
    stats_in,
    stats_wide,
    stats_wide_in,
    pair_send,
    pair_recv,
    rs_send,
    rs_recv,
    ag_send,
    ag_recv,
    fw_send,
    fw_recv,
    gz_send,
    gz_recv,
    st_send,
    st_recv,
    sz_send,
    sz_recv,
    gg_send,
    gg_recv,
    gf_send,
    gf_recv,
):
    d = lax.axis_index("dp")
    f = lax.axis_index("fsdp")
    chips = dp_count // 2
    q = d // 2
    core = d % 2
    rows = momentum.shape[0]
    width = momentum.shape[1] // CHUNKS
    partner = 2 * q + 1 - core

    barrier = pltpu.get_barrier_semaphore()
    for k in range(1, dp_count):
        pl.semaphore_signal(
            barrier, inc=1, device_id=(lax.rem(d + k, dp_count), f), device_id_type=MESH
        )
    for k in range(1, fsdp_count):
        pl.semaphore_signal(
            barrier, inc=1, device_id=(d, lax.rem(f + k, fsdp_count)), device_id_type=MESH
        )
    pl.semaphore_wait(barrier, dp_count + fsdp_count - 2)

    def send(source, target, send_sem, recv_sem, device):
        copy = pltpu.make_async_remote_copy(
            src_ref=source,
            dst_ref=target,
            send_sem=send_sem,
            recv_sem=recv_sem,
            device_id=device,
            device_id_type=MESH,
        )
        copy.start()
        return copy

    def block(device):
        return pl.ds(pl.multiple_of(device * rows, rows), rows)

    def chunk(h):
        return pl.ds(h * width, width)

    def ahead(k):
        return lax.rem(q + k, chips)

    def behind(k):
        return lax.rem(q + chips - k, chips)

    offsets = list(range(1, chips)) + [0]
    paired = {}
    for h in range(CHUNKS):
        for k in offsets:
            paired[h, k] = send(
                grad.at[block(2 * ahead(k) + 1 - core), chunk(h)],
                pair.at[h, k],
                pair_send.at[h, k],
                pair_recv.at[h, k],
                (partner, f),
            )
    scattered = {}
    for h in range(CHUNKS):
        for k in range(1, chips):
            paired[h, k].wait_recv()
            here = grad[block(2 * ahead(k) + core), chunk(h)].astype(jnp.float32)
            outgoing[h, k] = (here + pair[h, k].astype(jnp.float32)).astype(jnp.bfloat16)
            scattered[h, k] = send(
                outgoing.at[h, k],
                incoming.at[h, k],
                rs_send.at[h, k],
                rs_recv.at[h, k],
                (2 * ahead(k) + core, f),
            )
    gathered = {}
    forwarded = {}
    square_sum = jnp.float32(0.0)
    for h in range(CHUNKS):
        paired[h, 0].wait_recv()
        summed = grad[block(d), chunk(h)].astype(jnp.float32) + pair[h, 0].astype(jnp.float32)
        for k in range(1, chips):
            scattered[h, k].wait_recv()
            summed = summed + incoming[h, k].astype(jnp.float32)
        updated = momentum_decay * momentum[:, chunk(h)] + summed
        new_momentum[:, chunk(h)] = updated
        blended = summed + momentum_decay * updated
        columns[block(d), chunk(h)] = blended.astype(jnp.bfloat16)
        mine = columns.at[block(d), chunk(h)]
        for k in range(1, chips):
            gathered[h, k] = send(
                mine, mine, ag_send.at[h, k], ag_recv.at[h, k], (2 * ahead(k) + core, f)
            )
        forwarded[h, 0] = send(mine, mine, fw_send.at[h, 0], fw_recv.at[h, 0], (partner, f))
        square_sum = square_sum + jnp.sum(blended * blended)

    stats[0:8] = peaks[...]
    stats[8:16] = jnp.full((8, 128), square_sum, jnp.float32)
    stat_copies = [
        send(
            stats,
            stats_in.at[k],
            st_send.at[k],
            st_recv.at[k],
            (lax.rem(d + k, dp_count), f),
        )
        for k in range(1, dp_count)
    ]

    own_gram = jnp.zeros((rows, gram.shape[0]), jnp.float32)
    for h in range(CHUNKS):
        for k in range(1, chips):
            gathered[h, k].wait_recv()
            there = columns.at[block(2 * behind(k) + core), chunk(h)]
            forwarded[h, k] = send(
                there, there, fw_send.at[h, k], fw_recv.at[h, k], (partner, f)
            )
    for copy in stat_copies:
        copy.wait_recv()
    top = stats[0:8]
    level = stats[8:16]
    for k in range(1, dp_count):
        top = jnp.maximum(top, stats_in[k, 0:8])
        level = level + stats_in[k, 8:16]
    stats_wide[0:8] = top
    stats_wide[8:16] = level
    wide_copies = [
        send(
            stats_wide,
            stats_wide_in.at[k],
            sz_send.at[k],
            sz_recv.at[k],
            (d, lax.rem(f + k, fsdp_count)),
        )
        for k in range(1, fsdp_count)
    ]
    for h in range(CHUNKS):
        for k in range(chips):
            forwarded[h, k].wait_recv()
        own_gram = own_gram + lax.dot_general(
            columns[block(d), chunk(h)],
            columns[:, chunk(h)],
            (((1,), (1,)), ((), ())),
            preferred_element_type=jnp.float32,
        )

    gram_own[...] = own_gram.astype(jnp.bfloat16)
    gram_copies = [
        send(
            gram_own,
            gram_in.at[k],
            gz_send.at[k],
            gz_recv.at[k],
            (d, lax.rem(f + k, fsdp_count)),
        )
        for k in range(1, fsdp_count)
    ]
    for copy in wide_copies:
        copy.wait_recv()
    for k in range(1, fsdp_count):
        top = jnp.maximum(top, stats_wide_in[k, 0:8])
        level = level + stats_wide_in[k, 8:16]
    stats_out[0:8] = top
    stats_out[8:16] = level
    for copy in gram_copies:
        copy.wait_recv()
    for k in range(1, fsdp_count):
        own_gram = own_gram + gram_in[k].astype(jnp.float32)
    gram[block(d)] = own_gram.astype(jnp.bfloat16)
    mine = gram.at[block(d)]
    gram_gathered = {}
    gram_forwarded = {}
    for k in range(1, chips):
        gram_gathered[k] = send(
            mine, mine, gg_send.at[k], gg_recv.at[k], (2 * ahead(k) + core, f)
        )
    gram_forwarded[0] = send(mine, mine, gf_send.at[0], gf_recv.at[0], (partner, f))
    for k in range(1, chips):
        gram_gathered[k].wait_recv()
        there = gram.at[block(2 * behind(k) + core)]
        gram_forwarded[k] = send(there, there, gf_send.at[k], gf_recv.at[k], (partner, f))
    for k in range(chips):
        gram_forwarded[k].wait_recv()

    for group in (paired, scattered, gathered, forwarded, gram_gathered, gram_forwarded):
        for copy in group.values():
            copy.wait_send()
    for copy in stat_copies + wide_copies + gram_copies:
        copy.wait_send()


def reduce_and_gather(gradient, momentum, peaks):
    dp_count = lax.axis_size("dp")
    fsdp_count = lax.axis_size("fsdp")
    chips = dp_count // 2
    rows, shard_cols = momentum.shape
    width = shard_cols // CHUNKS
    in_vmem = pl.BlockSpec(memory_space=pltpu.VMEM)
    slots = pltpu.VMEM((CHUNKS, chips, rows, width), jnp.bfloat16)
    by_chunk = [pltpu.SemaphoreType.DMA((CHUNKS, chips))] * 8
    by_fsdp = [pltpu.SemaphoreType.DMA((fsdp_count,))] * 2
    by_dp = [pltpu.SemaphoreType.DMA((dp_count,))] * 2
    by_chip = [pltpu.SemaphoreType.DMA((chips,))] * 4
    return pl.pallas_call(
        functools.partial(exchange, dp_count, fsdp_count),
        out_shape=(
            jax.ShapeDtypeStruct((rows, shard_cols), jnp.float32),
            jax.ShapeDtypeStruct((KVL, shard_cols), jnp.bfloat16),
            jax.ShapeDtypeStruct((KVL, KVL), jnp.bfloat16),
            jax.ShapeDtypeStruct((16, 128), jnp.float32),
        ),
        in_specs=[in_vmem] * 3,
        out_specs=(in_vmem,) * 4,
        scratch_shapes=[
            slots,
            slots,
            slots,
            pltpu.VMEM((rows, KVL), jnp.bfloat16),
            pltpu.VMEM((fsdp_count, rows, KVL), jnp.bfloat16),
            pltpu.VMEM((16, 128), jnp.float32),
            pltpu.VMEM((dp_count, 16, 128), jnp.float32),
            pltpu.VMEM((16, 128), jnp.float32),
            pltpu.VMEM((fsdp_count, 16, 128), jnp.float32),
        ]
        + by_chunk
        + by_fsdp
        + by_dp
        + by_fsdp
        + by_chip,
        compiler_params=pltpu.CompilerParams(
            collective_id=0, has_side_effects=True, vmem_limit_bytes=40 * 1024 * 1024
        ),
    )(gradient, momentum, peaks)


def local(gradients, momentum, weight, logit_peaks, clip_threshold):
    peaks = jnp.zeros((8, 128), jnp.float32).at[:1, :HEADS].set(logit_peaks.astype(jnp.float32))
    new_momentum, columns, gram_total, stats = reduce_and_gather(gradients[0], momentum, peaks)
    largest = stats[0, :HEADS]
    square_total = stats[8, 0]
    update_norm = jnp.sqrt(square_total / (KVL * KVO)).reshape(1)
    inverse = 1.0 / (jnp.sqrt(square_total) + epsilon)
    gram = gram_total.astype(jnp.float32) * inverse * inverse
    whole = polynomial_of_gram(gram)
    orthogonal = inverse * jnp.dot(
        whole.astype(jnp.bfloat16), columns, preferred_element_type=jnp.float32
    )
    shard_cols = columns.shape[1]
    update_scale = update_gain * math.sqrt(max(KVL, KVO))
    stepped = weight - learning_rate * (update_scale * orthogonal + weight_decay * weight)
    factors = head_factors(largest, clip_threshold)
    shard_factors = lax.dynamic_slice_in_dim(
        factors, lax.axis_index("fsdp") * shard_cols, shard_cols
    )
    return (stepped * shard_factors[None, :], new_momentum, update_norm)


def solution(mesh):
    placed = (P("dp", None, "fsdp"), P("dp", "fsdp"), P(None, "fsdp"), P(("dp", "fsdp"), None), P())
    return jax.shard_map(
        local,
        mesh=mesh,
        in_specs=placed,
        out_specs=(P(None, "fsdp"), P("dp", "fsdp"), P()),
        check_vma=False,
    )
```

```python
import functools
import math

import jax
import jax.numpy as jnp
from jax import lax
from jax.experimental import pallas as pl
from jax.experimental.pallas import tpu as pltpu
from jax.sharding import PartitionSpec as P

KVL = 512
NOPE = 128
VDIM = 128
HEADS = 32
ITERS = 3
KVO = 8192


quintic_terms = (3.4445, -4.775, 2.0315)
learning_rate = 0.5
weight_decay = 0.1
momentum_decay = 0.95
update_gain = 0.2
epsilon = 1e-07


def head_factors(largest, clip_threshold):
    clip_ratio = jnp.minimum(1.0, clip_threshold.astype(jnp.float32)[0] / largest)
    key_scale = jnp.sqrt(clip_ratio)
    per_head = jnp.concatenate(
        [jnp.broadcast_to(key_scale[:, None], (HEADS, NOPE)), jnp.ones((HEADS, VDIM), jnp.float32)],
        axis=1,
    )
    return per_head.reshape(HEADS * (NOPE + VDIM))


def product(left, right):
    return jnp.dot(left, right, precision=lax.Precision.HIGH, preferred_element_type=jnp.float32)


def short_product(left, right):
    return jnp.dot(
        left.astype(jnp.bfloat16), right.astype(jnp.bfloat16), preferred_element_type=jnp.float32
    )


def polynomial_of_gram(gram_total, scale):
    lead, second, third = quintic_terms
    whole = None
    gram = gram_total.astype(jnp.float32) * scale
    square = scale * scale * jnp.dot(gram_total, gram_total, preferred_element_type=jnp.float32)
    for iteration in range(ITERS):
        multiply = product if iteration == ITERS - 1 else short_product
        rest = second * gram + third * (square if iteration == 0 else multiply(gram, gram))
        if whole is None:
            whole = lead * jnp.eye(KVL, dtype=jnp.float32) + rest
        else:
            whole = lead * whole + multiply(rest, whole)
        if iteration < ITERS - 1:
            half = lead * gram + multiply(rest, gram)
            gram = lead * half + multiply(half, rest)
    return whole


CHUNKS = 4
MESH = pl.DeviceIdType.MESH


def exchange(
    dp_count,
    fsdp_count,
    grad_all,
    momentum_all,
    peaks,
    new_momentum,
    columns,
    gram,
    stats_out,
    pair,
    outgoing,
    incoming,
    gram_own,
    gram_in,
    stats,
    stats_in,
    stats_wide,
    stats_wide_in,
    kept,
    momentum,
    kept_sem,
    momentum_sem,
    pair_send,
    pair_recv,
    rs_send,
    rs_recv,
    ag_send,
    ag_recv,
    fw_send,
    fw_recv,
    gz_send,
    gz_recv,
    st_send,
    st_recv,
    sz_send,
    sz_recv,
    gg_send,
    gg_recv,
    gf_send,
    gf_recv,
):
    d = lax.axis_index("dp")
    f = lax.axis_index("fsdp")
    chips = dp_count // 2
    q = d // 2
    core = d % 2
    rows = momentum.shape[0]
    width = momentum.shape[1] // CHUNKS
    partner = 2 * q + 1 - core

    kept_copies = []
    for k in range(chips):
        device = 2 * lax.rem(q + k, chips) + core
        source = grad_all.at[0, pl.ds(pl.multiple_of(device * rows, rows), rows)]
        kept_copies.append(pltpu.make_async_copy(source, kept.at[k], kept_sem.at[k]))
    momentum_copy = pltpu.make_async_copy(momentum_all, momentum, momentum_sem)
    for copy in kept_copies + [momentum_copy]:
        copy.start()

    barrier = pltpu.get_barrier_semaphore()
    for k in range(1, dp_count):
        pl.semaphore_signal(
            barrier, inc=1, device_id=(lax.rem(d + k, dp_count), f), device_id_type=MESH
        )
    for k in range(1, fsdp_count):
        pl.semaphore_signal(
            barrier, inc=1, device_id=(d, lax.rem(f + k, fsdp_count)), device_id_type=MESH
        )
    pl.semaphore_wait(barrier, dp_count + fsdp_count - 2)

    def send(source, target, send_sem, recv_sem, device):
        copy = pltpu.make_async_remote_copy(
            src_ref=source,
            dst_ref=target,
            send_sem=send_sem,
            recv_sem=recv_sem,
            device_id=device,
            device_id_type=MESH,
        )
        copy.start()
        return copy

    def block(device):
        return pl.ds(pl.multiple_of(device * rows, rows), rows)

    def chunk(h):
        return pl.ds(h * width, width)

    def ahead(k):
        return lax.rem(q + k, chips)

    def behind(k):
        return lax.rem(q + chips - k, chips)

    offsets = list(range(1, chips)) + [0]
    paired = {}
    for h in range(CHUNKS):
        for k in offsets:
            paired[h, k] = send(
                grad_all.at[0, block(2 * ahead(k) + 1 - core), chunk(h)],
                pair.at[h, k],
                pair_send.at[h, k],
                pair_recv.at[h, k],
                (partner, f),
            )
    scattered = {}
    for copy in kept_copies:
        copy.wait()
    for h in range(CHUNKS):
        for k in range(1, chips):
            paired[h, k].wait_recv()
            here = kept[k, :, chunk(h)].astype(jnp.float32)
            outgoing[h, k] = (here + pair[h, k].astype(jnp.float32)).astype(jnp.bfloat16)
            scattered[h, k] = send(
                outgoing.at[h, k],
                incoming.at[h, k],
                rs_send.at[h, k],
                rs_recv.at[h, k],
                (2 * ahead(k) + core, f),
            )
    gathered = {}
    forwarded = {}
    square_sum = jnp.float32(0.0)
    momentum_copy.wait()

    def forward(h):
        for k in range(1, chips):
            gathered[h, k].wait_recv()
            there = columns.at[block(2 * behind(k) + core), chunk(h)]
            forwarded[h, k] = send(
                there, there, fw_send.at[h, k], fw_recv.at[h, k], (partner, f)
            )

    for h in range(CHUNKS):
        paired[h, 0].wait_recv()
        summed = kept[0, :, chunk(h)].astype(jnp.float32) + pair[h, 0].astype(jnp.float32)
        for k in range(1, chips):
            scattered[h, k].wait_recv()
            summed = summed + incoming[h, k].astype(jnp.float32)
        updated = momentum_decay * momentum[:, chunk(h)] + summed
        new_momentum[:, chunk(h)] = updated
        blended = summed + momentum_decay * updated
        columns[block(d), chunk(h)] = blended.astype(jnp.bfloat16)
        mine = columns.at[block(d), chunk(h)]
        for k in range(1, chips):
            gathered[h, k] = send(
                mine, mine, ag_send.at[h, k], ag_recv.at[h, k], (2 * ahead(k) + core, f)
            )
        forwarded[h, 0] = send(mine, mine, fw_send.at[h, 0], fw_recv.at[h, 0], (partner, f))
        square_sum = square_sum + jnp.sum(blended * blended)
        if h >= 2:
            forward(h - 2)

    stats[0:8] = jnp.zeros((8, 128), jnp.float32)
    stats[0:1, 0:HEADS] = peaks[...].astype(jnp.float32)
    stats[8:16] = jnp.full((8, 128), square_sum, jnp.float32)
    stat_copies = [
        send(
            stats,
            stats_in.at[k],
            st_send.at[k],
            st_recv.at[k],
            (lax.rem(d + k, dp_count), f),
        )
        for k in range(1, dp_count)
    ]

    own_gram = jnp.zeros((rows, gram.shape[0]), jnp.float32)
    for h in range(max(CHUNKS - 2, 0), CHUNKS):
        forward(h)
    for copy in stat_copies:
        copy.wait_recv()
    top = stats[0:8]
    level = stats[8:16]
    for k in range(1, dp_count):
        top = jnp.maximum(top, stats_in[k, 0:8])
        level = level + stats_in[k, 8:16]
    stats_wide[0:8] = top
    stats_wide[8:16] = level
    wide_copies = [
        send(
            stats_wide,
            stats_wide_in.at[k],
            sz_send.at[k],
            sz_recv.at[k],
            (d, lax.rem(f + k, fsdp_count)),
        )
        for k in range(1, fsdp_count)
    ]
    for h in range(CHUNKS):
        for k in range(chips):
            forwarded[h, k].wait_recv()
        own_gram = own_gram + lax.dot_general(
            columns[block(d), chunk(h)],
            columns[:, chunk(h)],
            (((1,), (1,)), ((), ())),
            preferred_element_type=jnp.float32,
        )

    gram_own[...] = own_gram.astype(jnp.bfloat16)
    gram_copies = [
        send(
            gram_own,
            gram_in.at[k],
            gz_send.at[k],
            gz_recv.at[k],
            (d, lax.rem(f + k, fsdp_count)),
        )
        for k in range(1, fsdp_count)
    ]
    for copy in wide_copies:
        copy.wait_recv()
    for k in range(1, fsdp_count):
        top = jnp.maximum(top, stats_wide_in[k, 0:8])
        level = level + stats_wide_in[k, 8:16]
    stats_out[0:8] = top
    stats_out[8:16] = level
    for copy in gram_copies:
        copy.wait_recv()
    for k in range(1, fsdp_count):
        own_gram = own_gram + gram_in[k].astype(jnp.float32)
    gram[block(d)] = own_gram.astype(jnp.bfloat16)
    mine = gram.at[block(d)]
    gram_gathered = {}
    gram_forwarded = {}
    for k in range(1, chips):
        gram_gathered[k] = send(
            mine, mine, gg_send.at[k], gg_recv.at[k], (2 * ahead(k) + core, f)
        )
    gram_forwarded[0] = send(mine, mine, gf_send.at[0], gf_recv.at[0], (partner, f))
    for k in range(1, chips):
        gram_gathered[k].wait_recv()
        there = gram.at[block(2 * behind(k) + core)]
        gram_forwarded[k] = send(there, there, gf_send.at[k], gf_recv.at[k], (partner, f))
    for k in range(chips):
        gram_forwarded[k].wait_recv()

    for group in (paired, scattered, gathered, forwarded, gram_gathered, gram_forwarded):
        for copy in group.values():
            copy.wait_send()
    for copy in stat_copies + wide_copies + gram_copies:
        copy.wait_send()


def reduce_and_gather(gradient, momentum, peaks):
    dp_count = lax.axis_size("dp")
    fsdp_count = lax.axis_size("fsdp")
    chips = dp_count // 2
    rows, shard_cols = momentum.shape
    width = shard_cols // CHUNKS
    in_vmem = pl.BlockSpec(memory_space=pltpu.VMEM)
    slots = pltpu.VMEM((CHUNKS, chips, rows, width), jnp.bfloat16)
    by_chunk = [pltpu.SemaphoreType.DMA((CHUNKS, chips))] * 8
    by_fsdp = [pltpu.SemaphoreType.DMA((fsdp_count,))] * 2
    by_dp = [pltpu.SemaphoreType.DMA((dp_count,))] * 2
    by_chip = [pltpu.SemaphoreType.DMA((chips,))] * 4
    return pl.pallas_call(
        functools.partial(exchange, dp_count, fsdp_count),
        out_shape=(
            jax.ShapeDtypeStruct((rows, shard_cols), jnp.float32),
            jax.ShapeDtypeStruct((KVL, shard_cols), jnp.bfloat16),
            jax.ShapeDtypeStruct((KVL, KVL), jnp.bfloat16),
            jax.ShapeDtypeStruct((16, 128), jnp.float32),
        ),
        in_specs=[pl.BlockSpec(memory_space=pl.ANY)] * 2 + [in_vmem],
        out_specs=(in_vmem,) * 4,
        scratch_shapes=[
            slots,
            slots,
            slots,
            pltpu.VMEM((rows, KVL), jnp.bfloat16),
            pltpu.VMEM((fsdp_count, rows, KVL), jnp.bfloat16),
            pltpu.VMEM((16, 128), jnp.float32),
            pltpu.VMEM((dp_count, 16, 128), jnp.float32),
            pltpu.VMEM((16, 128), jnp.float32),
            pltpu.VMEM((fsdp_count, 16, 128), jnp.float32),
            pltpu.VMEM((chips, rows, shard_cols), jnp.bfloat16),
            pltpu.VMEM((rows, shard_cols), jnp.float32),
            pltpu.SemaphoreType.DMA((chips,)),
            pltpu.SemaphoreType.DMA,
        ]
        + by_chunk
        + by_fsdp
        + by_dp
        + by_fsdp
        + by_chip,
        compiler_params=pltpu.CompilerParams(
            collective_id=0, has_side_effects=True, vmem_limit_bytes=24 * 1024 * 1024
        ),
    )(gradient, momentum, peaks)


def local(gradients, momentum, weight, logit_peaks, clip_threshold):
    new_momentum, columns, gram_total, stats = reduce_and_gather(gradients, momentum, logit_peaks)
    largest = stats[0, :HEADS]
    square_total = stats[8, 0]
    update_norm = jnp.sqrt(square_total / (KVL * KVO)).reshape(1)
    inverse = 1.0 / (jnp.sqrt(square_total) + epsilon)
    whole = polynomial_of_gram(gram_total, inverse * inverse)
    orthogonal = inverse * jnp.dot(
        whole.astype(jnp.bfloat16), columns, preferred_element_type=jnp.float32
    )
    shard_cols = columns.shape[1]
    update_scale = update_gain * math.sqrt(max(KVL, KVO))
    stepped = weight - learning_rate * (update_scale * orthogonal + weight_decay * weight)
    factors = head_factors(largest, clip_threshold)
    shard_factors = lax.dynamic_slice_in_dim(
        factors, lax.axis_index("fsdp") * shard_cols, shard_cols
    )
    return (stepped * shard_factors[None, :], new_momentum, update_norm)


def solution(mesh):
    placed = (P("dp", None, "fsdp"), P("dp", "fsdp"), P(None, "fsdp"), P(("dp", "fsdp"), None), P())
    return jax.shard_map(
        local,
        mesh=mesh,
        in_specs=placed,
        out_specs=(P(None, "fsdp"), P("dp", "fsdp"), P()),
        check_vma=False,
    )
```

```python
import functools
import math

import jax
import jax.numpy as jnp
from jax import lax
from jax.experimental import pallas as pl
from jax.experimental.pallas import tpu as pltpu
from jax.sharding import PartitionSpec as P

KVL = 512
NOPE = 128
VDIM = 128
HEADS = 32
ITERS = 3
KVO = 8192


quintic_terms = (3.4445, -4.775, 2.0315)
learning_rate = 0.5
weight_decay = 0.1
momentum_decay = 0.95
update_gain = 0.2
epsilon = 1e-07


def head_factors(largest, clip_threshold):
    clip_ratio = jnp.minimum(1.0, clip_threshold.astype(jnp.float32)[0] / largest)
    key_scale = jnp.sqrt(clip_ratio)
    per_head = jnp.concatenate(
        [jnp.broadcast_to(key_scale[:, None], (HEADS, NOPE)), jnp.ones((HEADS, VDIM), jnp.float32)],
        axis=1,
    )
    return per_head.reshape(HEADS * (NOPE + VDIM))


def product(left, right):
    return jnp.dot(left, right, precision=lax.Precision.HIGH, preferred_element_type=jnp.float32)


def short_product(left, right):
    return jnp.dot(
        left.astype(jnp.bfloat16), right.astype(jnp.bfloat16), preferred_element_type=jnp.float32
    )


def polynomial_of_gram(gram_total, scale):
    lead, second, third = quintic_terms
    whole = None
    gram = gram_total.astype(jnp.float32) * scale
    square = scale * scale * jnp.dot(gram_total, gram_total, preferred_element_type=jnp.float32)
    for iteration in range(ITERS):
        multiply = product if iteration == ITERS - 1 else short_product
        rest = second * gram + third * (square if iteration == 0 else multiply(gram, gram))
        if whole is None:
            whole = lead * jnp.eye(KVL, dtype=jnp.float32) + rest
        else:
            whole = lead * whole + multiply(rest, whole)
        if iteration < ITERS - 1:
            half = lead * gram + multiply(rest, gram)
            gram = lead * half + multiply(half, rest)
    return whole


CHUNKS = 4
MESH = pl.DeviceIdType.MESH


def exchange(
    dp_count,
    fsdp_count,
    grad_all,
    momentum_all,
    peaks,
    new_momentum,
    columns,
    gram,
    stats_out,
    pair,
    outgoing,
    incoming,
    gram_own,
    gram_in,
    stats,
    stats_in,
    stats_wide,
    stats_wide_in,
    kept,
    momentum,
    kept_sem,
    momentum_sem,
    pair_send,
    pair_recv,
    rs_send,
    rs_recv,
    ag_send,
    ag_recv,
    fw_send,
    fw_recv,
    gz_send,
    gz_recv,
    st_send,
    st_recv,
    sz_send,
    sz_recv,
    gg_send,
    gg_recv,
    gf_send,
    gf_recv,
):
    d = lax.axis_index("dp")
    f = lax.axis_index("fsdp")
    chips = dp_count // 2
    q = d // 2
    core = d % 2
    rows = momentum.shape[0]
    width = momentum.shape[1] // CHUNKS
    partner = 2 * q + 1 - core

    barrier = pltpu.get_barrier_semaphore()
    for k in range(1, dp_count):
        pl.semaphore_signal(
            barrier, inc=1, device_id=(lax.rem(d + k, dp_count), f), device_id_type=MESH
        )
    for k in range(1, fsdp_count):
        pl.semaphore_signal(
            barrier, inc=1, device_id=(d, lax.rem(f + k, fsdp_count)), device_id_type=MESH
        )
    pl.semaphore_wait(barrier, dp_count + fsdp_count - 2)

    def send(source, target, send_sem, recv_sem, device):
        copy = pltpu.make_async_remote_copy(
            src_ref=source,
            dst_ref=target,
            send_sem=send_sem,
            recv_sem=recv_sem,
            device_id=device,
            device_id_type=MESH,
        )
        copy.start()
        return copy

    def block(device):
        return pl.ds(pl.multiple_of(device * rows, rows), rows)

    def chunk(h):
        return pl.ds(h * width, width)

    square_plane = chips == 4

    def ahead(k):
        if square_plane:
            return (q, q + 1 - 2 * (q % 2), q + 2 - 4 * (q // 2), 3 - q)[k]
        return lax.rem(q + k, chips)

    def behind(k):
        if square_plane:
            return ahead(k)
        return lax.rem(q + chips - k, chips)

    kept_copies = []
    for k in range(chips):
        source = grad_all.at[0, block(2 * ahead(k) + core)]
        kept_copies.append(pltpu.make_async_copy(source, kept.at[k], kept_sem.at[k]))
    momentum_copy = pltpu.make_async_copy(momentum_all, momentum, momentum_sem)
    for copy in kept_copies + [momentum_copy]:
        copy.start()

    offsets = list(range(1, chips)) + [0]
    paired = {}
    for h in range(CHUNKS):
        for k in offsets:
            paired[h, k] = send(
                grad_all.at[0, block(2 * ahead(k) + 1 - core), chunk(h)],
                pair.at[h, k],
                pair_send.at[h, k],
                pair_recv.at[h, k],
                (partner, f),
            )
    scattered = {}
    for copy in kept_copies:
        copy.wait()
    for h in range(CHUNKS):
        for k in range(1, chips):
            paired[h, k].wait_recv()
            here = kept[k, :, chunk(h)].astype(jnp.float32)
            outgoing[h, k] = (here + pair[h, k].astype(jnp.float32)).astype(jnp.bfloat16)
            scattered[h, k] = send(
                outgoing.at[h, k],
                incoming.at[h, k],
                rs_send.at[h, k],
                rs_recv.at[h, k],
                (2 * ahead(k) + core, f),
            )
    gathered = {}
    forwarded = {}
    square_sum = jnp.float32(0.0)
    momentum_copy.wait()

    def forward(h, which):
        for k in which:
            gathered[h, k].wait_recv()
            there = columns.at[block(2 * behind(k) + core), chunk(h)]
            if square_plane and k == 1 + h % 2:
                gathered[h, 3] = send(
                    there, there, ag_send.at[h, 3], ag_recv.at[h, 3], (2 * ahead(3 - k) + core, f)
                )
            forwarded[h, k] = send(
                there, there, fw_send.at[h, k], fw_recv.at[h, k], (partner, f)
            )

    direct = range(1, 3 if square_plane else chips)
    relayed = range(3, chips) if square_plane else ()
    for h in range(CHUNKS):
        paired[h, 0].wait_recv()
        summed = kept[0, :, chunk(h)].astype(jnp.float32) + pair[h, 0].astype(jnp.float32)
        for k in range(1, chips):
            scattered[h, k].wait_recv()
            summed = summed + incoming[h, k].astype(jnp.float32)
        updated = momentum_decay * momentum[:, chunk(h)] + summed
        new_momentum[:, chunk(h)] = updated
        blended = summed + momentum_decay * updated
        columns[block(d), chunk(h)] = blended.astype(jnp.bfloat16)
        mine = columns.at[block(d), chunk(h)]
        for k in direct:
            gathered[h, k] = send(
                mine, mine, ag_send.at[h, k], ag_recv.at[h, k], (2 * ahead(k) + core, f)
            )
        forwarded[h, 0] = send(mine, mine, fw_send.at[h, 0], fw_recv.at[h, 0], (partner, f))
        square_sum = square_sum + jnp.sum(blended * blended)
        if h >= 2:
            forward(h - 2, direct)

    stats[0:8] = jnp.zeros((8, 128), jnp.float32)
    stats[0:1, 0:HEADS] = peaks[...].astype(jnp.float32)
    stats[8:16] = jnp.full((8, 128), square_sum, jnp.float32)
    stat_copies = [
        send(
            stats,
            stats_in.at[k],
            st_send.at[k],
            st_recv.at[k],
            (lax.rem(d + k, dp_count), f),
        )
        for k in range(1, dp_count)
    ]

    own_gram = jnp.zeros((rows, gram.shape[0]), jnp.float32)
    for h in range(max(CHUNKS - 2, 0), CHUNKS):
        forward(h, direct)
    for h in range(CHUNKS):
        forward(h, relayed)
    for copy in stat_copies:
        copy.wait_recv()
    top = stats[0:8]
    level = stats[8:16]
    for k in range(1, dp_count):
        top = jnp.maximum(top, stats_in[k, 0:8])
        level = level + stats_in[k, 8:16]
    stats_wide[0:8] = top
    stats_wide[8:16] = level
    wide_copies = [
        send(
            stats_wide,
            stats_wide_in.at[k],
            sz_send.at[k],
            sz_recv.at[k],
            (d, lax.rem(f + k, fsdp_count)),
        )
        for k in range(1, fsdp_count)
    ]
    for h in range(CHUNKS):
        for k in range(chips):
            forwarded[h, k].wait_recv()
        own_gram = own_gram + lax.dot_general(
            columns[block(d), chunk(h)],
            columns[:, chunk(h)],
            (((1,), (1,)), ((), ())),
            preferred_element_type=jnp.float32,
        )

    gram_own[...] = own_gram.astype(jnp.bfloat16)
    gram_copies = [
        send(
            gram_own,
            gram_in.at[k],
            gz_send.at[k],
            gz_recv.at[k],
            (d, lax.rem(f + k, fsdp_count)),
        )
        for k in range(1, fsdp_count)
    ]
    for copy in wide_copies:
        copy.wait_recv()
    for k in range(1, fsdp_count):
        top = jnp.maximum(top, stats_wide_in[k, 0:8])
        level = level + stats_wide_in[k, 8:16]
    stats_out[0:8] = top
    stats_out[8:16] = level
    for copy in gram_copies:
        copy.wait_recv()
    for k in range(1, fsdp_count):
        own_gram = own_gram + gram_in[k].astype(jnp.float32)
    gram[block(d)] = own_gram.astype(jnp.bfloat16)
    mine = gram.at[block(d)]
    gram_gathered = {}
    gram_forwarded = {}
    for k in range(1, chips):
        gram_gathered[k] = send(
            mine, mine, gg_send.at[k], gg_recv.at[k], (2 * ahead(k) + core, f)
        )
    gram_forwarded[0] = send(mine, mine, gf_send.at[0], gf_recv.at[0], (partner, f))
    for k in range(1, chips):
        gram_gathered[k].wait_recv()
        there = gram.at[block(2 * behind(k) + core)]
        gram_forwarded[k] = send(there, there, gf_send.at[k], gf_recv.at[k], (partner, f))
    for k in range(chips):
        gram_forwarded[k].wait_recv()

    for group in (paired, scattered, gathered, forwarded, gram_gathered, gram_forwarded):
        for copy in group.values():
            copy.wait_send()
    for copy in stat_copies + wide_copies + gram_copies:
        copy.wait_send()


def reduce_and_gather(gradient, momentum, peaks):
    dp_count = lax.axis_size("dp")
    fsdp_count = lax.axis_size("fsdp")
    chips = dp_count // 2
    rows, shard_cols = momentum.shape
    width = shard_cols // CHUNKS
    in_vmem = pl.BlockSpec(memory_space=pltpu.VMEM)
    slots = pltpu.VMEM((CHUNKS, chips, rows, width), jnp.bfloat16)
    by_chunk = [pltpu.SemaphoreType.DMA((CHUNKS, chips))] * 8
    by_fsdp = [pltpu.SemaphoreType.DMA((fsdp_count,))] * 2
    by_dp = [pltpu.SemaphoreType.DMA((dp_count,))] * 2
    by_chip = [pltpu.SemaphoreType.DMA((chips,))] * 4
    return pl.pallas_call(
        functools.partial(exchange, dp_count, fsdp_count),
        out_shape=(
            jax.ShapeDtypeStruct((rows, shard_cols), jnp.float32),
            jax.ShapeDtypeStruct((KVL, shard_cols), jnp.bfloat16),
            jax.ShapeDtypeStruct((KVL, KVL), jnp.bfloat16),
            jax.ShapeDtypeStruct((16, 128), jnp.float32),
        ),
        in_specs=[pl.BlockSpec(memory_space=pl.ANY)] * 2 + [in_vmem],
        out_specs=(in_vmem,) * 4,
        scratch_shapes=[
            slots,
            slots,
            slots,
            pltpu.VMEM((rows, KVL), jnp.bfloat16),
            pltpu.VMEM((fsdp_count, rows, KVL), jnp.bfloat16),
            pltpu.VMEM((16, 128), jnp.float32),
            pltpu.VMEM((dp_count, 16, 128), jnp.float32),
            pltpu.VMEM((16, 128), jnp.float32),
            pltpu.VMEM((fsdp_count, 16, 128), jnp.float32),
            pltpu.VMEM((chips, rows, shard_cols), jnp.bfloat16),
            pltpu.VMEM((rows, shard_cols), jnp.float32),
            pltpu.SemaphoreType.DMA((chips,)),
            pltpu.SemaphoreType.DMA,
        ]
        + by_chunk
        + by_fsdp
        + by_dp
        + by_fsdp
        + by_chip,
        compiler_params=pltpu.CompilerParams(
            collective_id=0, has_side_effects=True, vmem_limit_bytes=24 * 1024 * 1024
        ),
    )(gradient, momentum, peaks)


def local(gradients, momentum, weight, logit_peaks, clip_threshold):
    new_momentum, columns, gram_total, stats = reduce_and_gather(gradients, momentum, logit_peaks)
    largest = stats[0, :HEADS]
    square_total = stats[8, 0]
    update_norm = jnp.sqrt(square_total / (KVL * KVO)).reshape(1)
    inverse = 1.0 / (jnp.sqrt(square_total) + epsilon)
    whole = polynomial_of_gram(gram_total, inverse * inverse)
    orthogonal = inverse * jnp.dot(
        whole.astype(jnp.bfloat16), columns, preferred_element_type=jnp.float32
    )
    shard_cols = columns.shape[1]
    update_scale = update_gain * math.sqrt(max(KVL, KVO))
    stepped = weight - learning_rate * (update_scale * orthogonal + weight_decay * weight)
    factors = head_factors(largest, clip_threshold)
    shard_factors = lax.dynamic_slice_in_dim(
        factors, lax.axis_index("fsdp") * shard_cols, shard_cols
    )
    return (stepped * shard_factors[None, :], new_momentum, update_norm)


def solution(mesh):
    placed = (P("dp", None, "fsdp"), P("dp", "fsdp"), P(None, "fsdp"), P(("dp", "fsdp"), None), P())
    return jax.shard_map(
        local,
        mesh=mesh,
        in_specs=placed,
        out_specs=(P(None, "fsdp"), P("dp", "fsdp"), P()),
        check_vma=False,
    )
```
